32 devices in a mesh: grp: 4 (over z), mem: 8 (over y, x, core).
Axes of the slice: x: 2, y: 2, z: 4, core: 2. Of those that a mesh axis runs over, the one named last changes fastest.
Arguments:
- volume: float32 [4, 8, 8, 512, 1024], P('grp', 'mem'), may hold values from -1 to 1
- transfer_coef: float32 [4, 4], replicated, may hold values from -3 to 3
- group_order: int32 [4], replicated, may hold values from 0 to 3, each once
- member_order: int32 [4, 8], replicated, may hold values from 0 to 7, each once within a row
- active_mask: int32 [4, 8], P('grp', 'mem'), may hold values 0 or 1
Outputs:
- picture: float32 [4, 512, 1024], P(None, 'mem', 'grp')
The draws below stay inside these ranges and needn't reach their ends.
All inputs are finite; a program needn't handle non-finite values. No bound on the sum of `active_mask` on one device may be relied on, other than what follows from the above.
Results may differ from the reference program's by a relative error of at most 0.0003.
Values sent between devices are 32-bit elements; how exact they have to be, the bound alone decides.
A program may use at most 192 MiB of HBM per device.

```python
import jax
import jax.numpy as jnp
from jax import lax

SAMPLES = 8
ROWS = 512
COLS = 1024
N_GRP = 4
N_MEM = 8


def touch_ends(result, own_key, smallest, top_value):
    longest = result.shape.index(max(result.shape))
    spots = []
    for shift in (0, 1):
        where = [jax.random.randint(jax.random.fold_in(own_key, axis), (), 0, length) for axis, length in enumerate(result.shape)]
        where[longest] = (where[longest] + shift) % result.shape[longest]
        spots.append(tuple(where))
    return result.at[spots[0]].set(smallest).at[spots[1]].set(top_value)


def steps_of(stream_key, dims, shards, low, top_value):
    loudness, own = 1.0, jax.random.fold_in(stream_key, 6)
    for axis_at, shards_of in shards:
        steps = jnp.exp(jax.random.uniform(jax.random.fold_in(own, axis_at), (shards_of,), jnp.float32, low / len(shards), top_value / len(shards)))
        loudness = loudness * jnp.repeat(steps, dims[axis_at] // shards_of).reshape([-1 if axis == axis_at else 1 for axis in range(len(dims))])
    return loudness


def gaussian(stream_key, extent, width, reach, kind=jnp.bfloat16):
    values = jax.random.normal(stream_key, extent, jnp.float32) * width
    return jnp.minimum(jnp.maximum(values, -reach), reach).astype(kind)


def setup_inputs(seed: int = 0) -> dict:
    key_of = jax.random.split(jax.random.key(seed), 6)
    return {
        "volume": jnp.clip(jax.random.uniform(key_of[0], (N_GRP, N_MEM, SAMPLES, ROWS, COLS), jnp.float32, -1.0, 1.0) * steps_of(key_of[0], (N_GRP, N_MEM, SAMPLES, ROWS, COLS), ((0, 4), (1, 8)), -0.4, 0.0), -1.0, 1.0),
        "transfer_coef": gaussian(key_of[1], (4, 4), 0.6, 3.0, jnp.float32),
        "group_order": jax.random.permutation(key_of[2], N_GRP).astype(jnp.int32),
        "member_order": jax.vmap(lambda own: jax.random.permutation(own, N_MEM))(jax.random.split(key_of[3], N_GRP)).reshape((N_GRP, N_MEM)).astype(jnp.int32),
        "active_mask": touch_ends((jax.random.randint(key_of[4], (N_GRP, N_MEM), 0, 4) < 3).astype(jnp.int32), jax.random.fold_in(key_of[4], 1), 0, 1),
    }


def polynomial(coef_row, values):
    return coef_row[0] + values * (coef_row[1] + values * (coef_row[2] + values * coef_row[3]))


def march_brick(samples, transfer_coef, active_flag):
    density_scale = 3.0 / (SAMPLES * N_GRP * N_MEM)

    def march_step(state_pair, values):
        optical_depth, colour = state_pair
        extinction = polynomial(transfer_coef[3], values) ** 2 * density_scale
        opacity = 1.0 - jnp.exp(-extinction)
        tinted = jax.nn.sigmoid(jnp.stack([polynomial(transfer_coef[channel], values) for channel in range(3)]))
        colour = colour + (jnp.exp(-optical_depth) * opacity)[None] * tinted
        return (optical_depth + extinction, colour), None

    start = (jnp.zeros(samples.shape[1:], jnp.float32), jnp.zeros((3,) + samples.shape[1:], jnp.float32))
    (optical_depth, colour), unused = lax.scan(march_step, start, samples)
    coverage = 1.0 - jnp.exp(-optical_depth)
    return jnp.concatenate([colour, coverage[None]], 0) * active_flag


def reference(volume, transfer_coef, group_order, member_order, active_mask):
    global_rank = (group_order[:, None] * N_MEM + member_order).reshape(-1).astype(jnp.int32)
    total = N_GRP * N_MEM
    positions = jnp.arange(total, dtype=jnp.int32)
    inverse = jnp.sum(positions[:, None] * (global_rank[:, None] == positions[None, :]).astype(jnp.int32), axis=0).astype(jnp.int32)

    def composite_step(picture, brick_index):
        group_index = brick_index // N_MEM
        member_index = brick_index % N_MEM
        samples = volume[group_index, member_index]
        active_flag = active_mask[group_index, member_index].astype(jnp.float32)
        layer = march_brick(samples, transfer_coef, active_flag)
        return picture + (1.0 - picture[3:4]) * layer, None

    picture, unused = lax.scan(composite_step, jnp.zeros((4, ROWS, COLS), jnp.float32), inverse)
    return picture
```

```python
import functools
import math

import jax
import jax.numpy as jnp
from jax import lax
from jax.experimental import pallas as pl
from jax.experimental.pallas import tpu as pltpu
from jax.sharding import PartitionSpec as P

MESH = pl.DeviceIdType.MESH
CHUNKS = 4
TILE_ROWS = 8


def kernel(groups, members, coef_ref, group_ref, member_ref, active_ref, volume_ref, out_ref,
           vol, tloc, tin, col, pcol, mout, min_, tnear, tslab, sout, sin, zout, zin,
           vol_sem, t_send, t_recv, c_send, c_recv, m_send, m_recv, s_send, s_recv, z_send, z_recv):
    chunks, _, samples, rows, cols = vol.shape
    block_rows = chunks * rows
    chips = members // 2
    group_cols = cols // groups
    g = lax.axis_index("grp")
    me = lax.axis_index("mem")
    chip = me // 2
    core = me % 2
    partner = me + 1 - 2 * core
    row_tiles = rows // TILE_ROWS

    def fetch(j, d):
        start = pl.multiple_of(d * block_rows + j * rows, TILE_ROWS)
        return pltpu.make_async_copy(
            volume_ref.at[0, 0, :, pl.ds(start, rows), :], vol.at[j, d], vol_sem.at[j, d])

    def send_t(j, d, src):
        return pltpu.make_async_remote_copy(
            tloc.at[j, d], tin.at[j, src], t_send.at[j, d], t_recv.at[j, src],
            device_id={"mem": d}, device_id_type=MESH)

    def send_col(j, k):
        return pltpu.make_async_remote_copy(
            col.at[j, 2 * k + 1 - core], pcol.at[j, k], c_send.at[j, k], c_recv.at[j, k],
            device_id={"mem": partner}, device_id_type=MESH)

    def send_m(j, k, src):
        return pltpu.make_async_remote_copy(
            mout.at[j, k], min_.at[j, src], m_send.at[j, k], m_recv.at[j, src],
            device_id={"mem": 2 * k + core}, device_id_type=MESH)

    def send_s(j, k, src):
        return pltpu.make_async_remote_copy(
            sout.at[j, k], sin.at[j, src], s_send.at[j, k], s_recv.at[j, src],
            device_id={"mem": 2 * k + core}, device_id_type=MESH)

    def send_z(j, k, src):
        return pltpu.make_async_remote_copy(
            zout.at[j, k], zin.at[j, src], z_send.at[j, k], z_recv.at[j, src],
            device_id={"grp": k}, device_id_type=MESH)

    def each(count, fn):
        def step(i, carry):
            fn(i)
            return carry
        lax.fori_loop(0, count, step, 0)

    each(chunks, lambda j: each(members, lambda off: fetch(j, (me + 1 + off) % members).start()))

    barrier = pltpu.get_barrier_semaphore()
    each(members - 1, lambda off: pl.semaphore_signal(
        barrier, inc=1, device_id={"mem": (me + 1 + off) % members}, device_id_type=MESH))
    each(groups - 1, lambda off: pl.semaphore_signal(
        barrier, inc=1, device_id={"grp": (g + 1 + off) % groups}, device_id_type=MESH))
    pl.semaphore_wait(barrier, members + groups - 2)

    density_factor = math.sqrt(3.0 / (samples * groups * members) * math.log2(math.e))
    coef = [[coef_ref[c, p] * (0.5 if c < 3 else density_factor) for p in range(4)] for c in range(4)]
    active = active_ref[0, 0].astype(jnp.float32)
    half_active = active * 0.5
    width = min(256, cols)
    col_tiles = cols // width
    ranks = [member_ref[g, i] for i in range(members)]
    near = [jnp.minimum(ranks[2 * q], ranks[2 * q + 1]) for q in range(chips)]
    far = [jnp.maximum(ranks[2 * q], ranks[2 * q + 1]) for q in range(chips)]
    own_first = member_ref[g, me] < member_ref[g, partner]
    orders = [group_ref[i] for i in range(groups)]

    def tiles(fn, count=None):
        def step(i, carry):
            row = pl.ds(pl.multiple_of((i // col_tiles) * TILE_ROWS, TILE_ROWS), TILE_ROWS)
            column = pl.ds(pl.multiple_of((i % col_tiles) * width, width), width)
            fn(row, column)
            return carry
        lax.fori_loop(0, row_tiles * col_tiles, step, 0)

    def march(j, d):
        def tile(row, column):
            depth = jnp.zeros((TILE_ROWS, width), jnp.float32)
            light = jnp.ones((TILE_ROWS, width), jnp.float32)
            colour = [jnp.zeros((TILE_ROWS, width), jnp.float32) for _ in range(3)]
            for k in range(samples):
                v = vol[j, d, k, row, column]
                poly = [q[0] + v * (q[1] + v * (q[2] + v * q[3])) for q in coef]
                depth = depth - poly[3] * poly[3]
                after = jnp.exp2(depth)
                weight = light - after
                light = after
                colour = [colour[c] + weight * jnp.tanh(poly[c]) for c in range(3)]
            coverage = 1.0 - light
            tloc[j, d, row, column] = 1.0 - active * coverage
            for c in range(3):
                col[j, d, c, row, column] = half_active * (coverage + colour[c])
        tiles(tile)

    def produce(j):
        def unit(off):
            d = (me + 1 + off) % members
            fetch(j, d).wait()
            march(j, d)

            @pl.when(off < members - 1)
            def _():
                send_t(j, d, me).start()

            @pl.when(d % 2 != core)
            def _():
                send_col(j, d // 2).start()
        each(members, unit)

        def keep(row, column):
            tin[j, me, row, column] = tloc[j, me, row, column]
        tiles(keep)

    def ratios(j):
        def arrive(off):
            i = (me + 1 + off) % members
            send_t(j, i, i).wait_recv()
        each(members - 1, arrive)

        def tile(row, column):
            t = [tin[j, i, row, column] for i in range(members)]
            total = t[0]
            for i in range(1, members):
                total = total * t[i]
            tslab[j, row, column] = total
            for q in range(chips):
                before = jnp.ones((TILE_ROWS, width), jnp.float32)
                between = jnp.ones((TILE_ROWS, width), jnp.float32)
                for i in range(members):
                    nearer = ranks[i] < near[q]
                    inside = jnp.logical_and(ranks[i] >= near[q], ranks[i] < far[q])
                    before = before * jnp.where(nearer, t[i], 1.0)
                    between = between * jnp.where(inside, t[i], 1.0)
                tnear[j, q, row, column] = before
                mout[j, q, row, column] = between
        tiles(tile)
        each(chips - 1, lambda off: send_m(j, (chip + 1 + off) % chips, chip).start())

        def keep(row, column):
            min_[j, chip, row, column] = mout[j, chip, row, column]
        tiles(keep)

    def pair_sums(j):
        def unit(off):
            k = (chip + 1 + off) % chips

            @pl.when(off < chips - 1)
            def _():
                send_m(j, k, k).wait_recv()
            send_col(j, k).wait_recv()

            def tile(row, column):
                ratio = min_[j, k, row, column]
                own_factor = jnp.where(own_first, 1.0, ratio)
                other_factor = jnp.where(own_first, ratio, 1.0)
                for c in range(3):
                    sout[j, k, c, row, column] = (
                        col[j, 2 * k + core, c, row, column] * own_factor
                        + pcol[j, k, c, row, column] * other_factor)
            tiles(tile)

            @pl.when(off < chips - 1)
            def _():
                send_s(j, k, chip).start()
        each(chips, unit)

        def keep(row, column):
            for c in range(3):
                sin[j, chip, c, row, column] = sout[j, chip, c, row, column]
        tiles(keep)

    def slab(j):
        def arrive(off):
            q = (chip + 1 + off) % chips
            send_s(j, q, q).wait_recv()
        each(chips - 1, arrive)

        def part(k):
            def tile(i):
                row = pl.ds(pl.multiple_of(i * TILE_ROWS, TILE_ROWS), TILE_ROWS)
                column = pl.ds(pl.multiple_of(k * group_cols, group_cols), group_cols)
                factor = [tnear[j, q, row, column] for q in range(chips)]
                for c in range(3):
                    total = factor[0] * sin[j, 0, c, row, column]
                    for q in range(1, chips):
                        total = total + factor[q] * sin[j, q, c, row, column]
                    zout[j, k, c, row, :] = total
                zout[j, k, 3, row, :] = tslab[j, row, column]
            each(row_tiles, tile)

        def unit(off):
            k = (g + 1 + off) % groups
            part(k)

            @pl.when(off < groups - 1)
            def _():
                send_z(j, k, g).start()
        each(groups, unit)
        zin[j, g] = zout[j, g]

    def finish(j):
        def arrive(off):
            i = (g + 1 + off) % groups
            send_z(j, i, i).wait_recv()
        each(groups - 1, arrive)
        for r in range(row_tiles):
            row = pl.ds(r * TILE_ROWS, TILE_ROWS)
            out_row = pl.ds(pl.multiple_of(j * rows + r * TILE_ROWS, TILE_ROWS), TILE_ROWS)
            t = [zin[j, i, 3, row, :] for i in range(groups)]
            total = t[0]
            for i in range(1, groups):
                total = total * t[i]
            out_ref[3, out_row, :] = 1.0 - total
            factor = []
            for i in range(groups):
                before = jnp.ones_like(total)
                for o in range(groups):
                    if o != i:
                        before = before * jnp.where(orders[o] < orders[i], t[o], 1.0)
                factor.append(before)
            for c in range(3):
                colour = factor[0] * zin[j, 0, c, row, :]
                for i in range(1, groups):
                    colour = colour + factor[i] * zin[j, i, c, row, :]
                out_ref[c, out_row, :] = colour

    def step(s):
        for lag, stage in enumerate((produce, ratios, pair_sums, slab, finish)):
            @pl.when(jnp.logical_and(s >= lag, s < chunks + lag))
            def _():
                stage(s - lag)
    each(chunks + 4, step)

    def drain(j):
        each(members - 1, lambda off: send_t(j, (me + 1 + off) % members, me).wait_send())
        each(chips, lambda k: send_col(j, k).wait_send())
        each(chips - 1, lambda off: send_m(j, (chip + 1 + off) % chips, chip).wait_send())
        each(chips - 1, lambda off: send_s(j, (chip + 1 + off) % chips, chip).wait_send())
        each(groups - 1, lambda off: send_z(j, (g + 1 + off) % groups, g).wait_send())
    each(chunks, drain)


def solution(mesh):
    groups, members = mesh.shape["grp"], mesh.shape["mem"]
    chips = members // 2

    def body(volume, transfer_coef, group_order, member_order, active_mask):
        samples, image_rows, cols = volume.shape[2:]
        block_rows = image_rows // members
        chunks = min(CHUNKS, block_rows // TILE_ROWS)
        rows = block_rows // chunks
        group_cols = cols // groups
        smem = pl.BlockSpec(memory_space=pltpu.SMEM)
        f32 = jnp.float32
        dma = pltpu.SemaphoreType.DMA
        scratch = [
            pltpu.VMEM((chunks, members, samples, rows, cols), f32),
            pltpu.VMEM((chunks, members, rows, cols), f32),
            pltpu.VMEM((chunks, members, rows, cols), f32),
            pltpu.VMEM((chunks, members, 3, rows, cols), f32),
            pltpu.VMEM((chunks, chips, 3, rows, cols), f32),
            pltpu.VMEM((chunks, chips, rows, cols), f32),
            pltpu.VMEM((chunks, chips, rows, cols), f32),
            pltpu.VMEM((chunks, chips, rows, cols), f32),
            pltpu.VMEM((chunks, rows, cols), f32),
            pltpu.VMEM((chunks, chips, 3, rows, cols), f32),
            pltpu.VMEM((chunks, chips, 3, rows, cols), f32),
            pltpu.VMEM((chunks, groups, 4, rows, group_cols), f32),
            pltpu.VMEM((chunks, groups, 4, rows, group_cols), f32),
            dma((chunks, members)),
            dma((chunks, members)), dma((chunks, members)),
            dma((chunks, chips)), dma((chunks, chips)),
            dma((chunks, chips)), dma((chunks, chips)),
            dma((chunks, chips)), dma((chunks, chips)),
            dma((chunks, groups)), dma((chunks, groups)),
        ]
        return pl.pallas_call(
            functools.partial(kernel, groups, members),
            out_shape=jax.ShapeDtypeStruct((4, block_rows, group_cols), f32),
            in_specs=[smem, smem, smem, smem, pl.BlockSpec(memory_space=pl.ANY)],
            out_specs=pl.BlockSpec(memory_space=pltpu.VMEM),
            scratch_shapes=scratch,
            compiler_params=pltpu.CompilerParams(
                collective_id=0, has_side_effects=True, vmem_limit_bytes=60 * 1024 * 1024),
        )(transfer_coef, group_order, member_order, active_mask, volume)

    in_specs = (P("grp", "mem", None, None, None), P(), P(), P(), P("grp", "mem"))
    out_specs = P(None, "mem", "grp")
    return jax.shard_map(body, mesh=mesh, in_specs=in_specs, out_specs=out_specs, check_vma=False)
```

```python
import functools
import math

import jax
import jax.numpy as jnp
from jax import lax
from jax.experimental import pallas as pl
from jax.experimental.pallas import tpu as pltpu
from jax.sharding import PartitionSpec as P

MESH = pl.DeviceIdType.MESH
CHUNKS = 4
EARLY = 3
TILE_ROWS = 8


def kernel(groups, members, coef_ref, group_ref, member_ref, active_ref, volume_ref, out_ref,
           vol, tloc, tin, col, pcol, mout, min_, tnear, tslab, sout, sin, zout, zin,
           vol_sem, t_send, t_recv, c_send, c_recv, m_send, m_recv, s_send, s_recv, z_send, z_recv):
    chunks, _, samples, rows, cols = vol.shape
    block_rows = chunks * rows
    chips = members // 2
    group_cols = cols // groups
    g = lax.axis_index("grp")
    me = lax.axis_index("mem")
    chip = me // 2
    core = me % 2
    partner = me + 1 - 2 * core
    row_tiles = rows // TILE_ROWS

    def fetch(j, d):
        start = pl.multiple_of(d * block_rows + j * rows, TILE_ROWS)
        return pltpu.make_async_copy(
            volume_ref.at[0, 0, :, pl.ds(start, rows), :], vol.at[j, d], vol_sem.at[j])

    def send_t(j, d, src):
        return pltpu.make_async_remote_copy(
            tloc.at[j, d], tin.at[j, src], t_send, t_recv.at[j],
            device_id={"mem": d}, device_id_type=MESH)

    def send_col(j, k):
        return pltpu.make_async_remote_copy(
            col.at[j, 2 * k + 1 - core], pcol.at[j, k], c_send, c_recv.at[j],
            device_id={"mem": partner}, device_id_type=MESH)

    def send_m(j, k, src):
        return pltpu.make_async_remote_copy(
            mout.at[j, k], min_.at[j, src], m_send, m_recv.at[j],
            device_id={"mem": 2 * k + core}, device_id_type=MESH)

    def send_s(j, k, src):
        return pltpu.make_async_remote_copy(
            sout.at[j, k], sin.at[j, src], s_send, s_recv.at[j],
            device_id={"mem": 2 * k + core}, device_id_type=MESH)

    def send_z(j, k, src):
        return pltpu.make_async_remote_copy(
            zout.at[j, k], zin.at[j, src], z_send, z_recv.at[j],
            device_id={"grp": k}, device_id_type=MESH)

    def landed(ref, sem):
        pltpu.make_async_copy(ref, ref, sem).wait()

    def each(count, fn):
        def step(i, carry):
            fn(i)
            return carry
        lax.fori_loop(0, count, step, 0)

    each(chunks, lambda j: each(members, lambda off: fetch(j, (me + 1 + off) % members).start()))

    barrier = pltpu.get_barrier_semaphore()
    each(members - 1, lambda off: pl.semaphore_signal(
        barrier, inc=1, device_id={"mem": (me + 1 + off) % members}, device_id_type=MESH))
    each(groups - 1, lambda off: pl.semaphore_signal(
        barrier, inc=1, device_id={"grp": (g + 1 + off) % groups}, device_id_type=MESH))

    density_factor = math.sqrt(3.0 / (samples * groups * members) * math.log2(math.e))
    coef = [[coef_ref[c, p] * (0.5 if c < 3 else density_factor) for p in range(4)] for c in range(4)]
    active = active_ref[0, 0].astype(jnp.float32)
    half_active = active * 0.5
    width = min(512, cols)
    col_tiles = cols // width
    ranks = [member_ref[g, i] for i in range(members)]
    near = [jnp.minimum(ranks[2 * q], ranks[2 * q + 1]) for q in range(chips)]
    far = [jnp.maximum(ranks[2 * q], ranks[2 * q + 1]) for q in range(chips)]
    own_first = member_ref[g, me] < member_ref[g, partner]
    orders = [group_ref[i] for i in range(groups)]

    def tiles(fn, count=None):
        def step(i, carry):
            row = pl.ds(pl.multiple_of((i // col_tiles) * TILE_ROWS, TILE_ROWS), TILE_ROWS)
            column = pl.ds(pl.multiple_of((i % col_tiles) * width, width), width)
            fn(row, column)
            return carry
        lax.fori_loop(0, row_tiles * col_tiles, step, 0)

    def march(j, d):
        def tile(row, column):
            depth = jnp.zeros((TILE_ROWS, width), jnp.float32)
            light = jnp.ones((TILE_ROWS, width), jnp.float32)
            colour = [jnp.zeros((TILE_ROWS, width), jnp.float32) for _ in range(3)]
            for k in range(samples):
                v = vol[j, d, k, row, column]
                poly = [q[0] + v * (q[1] + v * (q[2] + v * q[3])) for q in coef]
                depth = depth - poly[3] * poly[3]
                after = jnp.exp2(depth)
                weight = light - after
                light = after
                colour = [colour[c] + weight * jnp.tanh(poly[c]) for c in range(3)]
            coverage = 1.0 - light
            tloc[j, d, row, column] = 1.0 - active * coverage
            for c in range(3):
                col[j, d, c, row, column] = half_active * (coverage + colour[c])
        tiles(tile)

    early = min(EARLY, members - 1)

    def produce(j):
        @pl.when(j > 0)
        def _():
            landed(vol.at[j], vol_sem.at[j])

        def unit(off):
            d = (me + 1 + off) % members

            @pl.when(jnp.logical_or(j > 0, off >= early))
            def _():
                march(j, d)

            @pl.when(off < members - 1)
            def _():
                send_t(j, d, me).start()

            @pl.when(d % 2 != core)
            def _():
                send_col(j, d // 2).start()
        each(members, unit)

        def keep(row, column):
            tin[j, me, row, column] = tloc[j, me, row, column]
        tiles(keep)

    def ratios(j):
        landed(tin.at[j, pl.ds(0, members - 1)], t_recv.at[j])

        def tile(row, column):
            t = [tin[j, i, row, column] for i in range(members)]
            total = t[0]
            for i in range(1, members):
                total = total * t[i]
            tslab[j, row, column] = total
            for q in range(chips):
                before = jnp.ones((TILE_ROWS, width), jnp.float32)
                between = jnp.ones((TILE_ROWS, width), jnp.float32)
                for i in range(members):
                    nearer = ranks[i] < near[q]
                    inside = jnp.logical_and(ranks[i] >= near[q], ranks[i] < far[q])
                    before = before * jnp.where(nearer, t[i], 1.0)
                    between = between * jnp.where(inside, t[i], 1.0)
                tnear[j, q, row, column] = before
                mout[j, q, row, column] = between
        tiles(tile)
        each(chips - 1, lambda off: send_m(j, (chip + 1 + off) % chips, chip).start())

        def keep(row, column):
            min_[j, chip, row, column] = mout[j, chip, row, column]
        tiles(keep)

    def pair_sums(j):
        landed(min_.at[j, pl.ds(0, chips - 1)], m_recv.at[j])
        landed(pcol.at[j], c_recv.at[j])

        def unit(off):
            k = (chip + 1 + off) % chips

            def tile(row, column):
                ratio = min_[j, k, row, column]
                own_factor = jnp.where(own_first, 1.0, ratio)
                other_factor = jnp.where(own_first, ratio, 1.0)
                for c in range(3):
                    sout[j, k, c, row, column] = (
                        col[j, 2 * k + core, c, row, column] * own_factor
                        + pcol[j, k, c, row, column] * other_factor)
            tiles(tile)

            @pl.when(off < chips - 1)
            def _():
                send_s(j, k, chip).start()
        each(chips, unit)

        def keep(row, column):
            for c in range(3):
                sin[j, chip, c, row, column] = sout[j, chip, c, row, column]
        tiles(keep)

    def slab(j):
        landed(sin.at[j, pl.ds(0, chips - 1)], s_recv.at[j])

        def part(k):
            def tile(i):
                row = pl.ds(pl.multiple_of(i * TILE_ROWS, TILE_ROWS), TILE_ROWS)
                column = pl.ds(pl.multiple_of(k * group_cols, group_cols), group_cols)
                factor = [tnear[j, q, row, column] for q in range(chips)]
                for c in range(3):
                    total = factor[0] * sin[j, 0, c, row, column]
                    for q in range(1, chips):
                        total = total + factor[q] * sin[j, q, c, row, column]
                    zout[j, k, c, row, :] = total
                zout[j, k, 3, row, :] = tslab[j, row, column]
            each(row_tiles, tile)

        def unit(off):
            k = (g + 1 + off) % groups
            part(k)

            @pl.when(off < groups - 1)
            def _():
                send_z(j, k, g).start()
        each(groups, unit)
        zin[j, g] = zout[j, g]

    def finish(j):
        landed(zin.at[j, pl.ds(0, groups - 1)], z_recv.at[j])
        for r in range(row_tiles):
            row = pl.ds(r * TILE_ROWS, TILE_ROWS)
            out_row = pl.ds(pl.multiple_of(j * rows + r * TILE_ROWS, TILE_ROWS), TILE_ROWS)
            t = [zin[j, i, 3, row, :] for i in range(groups)]
            total = t[0]
            for i in range(1, groups):
                total = total * t[i]
            out_ref[3, out_row, :] = 1.0 - total
            factor = []
            for i in range(groups):
                before = jnp.ones_like(total)
                for o in range(groups):
                    if o != i:
                        before = before * jnp.where(orders[o] < orders[i], t[o], 1.0)
                factor.append(before)
            for c in range(3):
                colour = factor[0] * zin[j, 0, c, row, :]
                for i in range(1, groups):
                    colour = colour + factor[i] * zin[j, i, c, row, :]
                out_ref[c, out_row, :] = colour

    def step(s):
        for lag, stage in enumerate((produce, ratios, pair_sums, slab, finish)):
            @pl.when(jnp.logical_and(s >= lag, s < chunks + lag))
            def _():
                stage(s - lag)
    landed(vol.at[0], vol_sem.at[0])
    each(early, lambda off: march(0, (me + 1 + off) % members))
    pl.semaphore_wait(barrier, members + groups - 2)
    each(chunks + 4, step)

    landed(tloc.at[:, pl.ds(0, members - 1)], t_send)
    landed(pcol, c_send)
    landed(mout.at[:, pl.ds(0, chips - 1)], m_send)
    landed(sout.at[:, pl.ds(0, chips - 1)], s_send)
    landed(zout.at[:, pl.ds(0, groups - 1)], z_send)


def solution(mesh):
    groups, members = mesh.shape["grp"], mesh.shape["mem"]
    chips = members // 2

    def body(volume, transfer_coef, group_order, member_order, active_mask):
        samples, image_rows, cols = volume.shape[2:]
        block_rows = image_rows // members
        chunks = min(CHUNKS, block_rows // TILE_ROWS)
        rows = block_rows // chunks
        group_cols = cols // groups
        smem = pl.BlockSpec(memory_space=pltpu.SMEM)
        f32 = jnp.float32
        dma = pltpu.SemaphoreType.DMA
        scratch = [
            pltpu.VMEM((chunks, members, samples, rows, cols), f32),
            pltpu.VMEM((chunks, members, rows, cols), f32),
            pltpu.VMEM((chunks, members, rows, cols), f32),
            pltpu.VMEM((chunks, members, 3, rows, cols), f32),
            pltpu.VMEM((chunks, chips, 3, rows, cols), f32),
            pltpu.VMEM((chunks, chips, rows, cols), f32),
            pltpu.VMEM((chunks, chips, rows, cols), f32),
            pltpu.VMEM((chunks, chips, rows, cols), f32),
            pltpu.VMEM((chunks, rows, cols), f32),
            pltpu.VMEM((chunks, chips, 3, rows, cols), f32),
            pltpu.VMEM((chunks, chips, 3, rows, cols), f32),
            pltpu.VMEM((chunks, groups, 4, rows, group_cols), f32),
            pltpu.VMEM((chunks, groups, 4, rows, group_cols), f32),
            dma((chunks,)),
            dma, dma((chunks,)),
            dma, dma((chunks,)),
            dma, dma((chunks,)),
            dma, dma((chunks,)),
            dma, dma((chunks,)),
        ]
        return pl.pallas_call(
            functools.partial(kernel, groups, members),
            out_shape=jax.ShapeDtypeStruct((4, block_rows, group_cols), f32),
            in_specs=[smem, smem, smem, smem, pl.BlockSpec(memory_space=pl.ANY)],
            out_specs=pl.BlockSpec(memory_space=pltpu.VMEM),
            scratch_shapes=scratch,
            compiler_params=pltpu.CompilerParams(
                collective_id=0, has_side_effects=True, vmem_limit_bytes=60 * 1024 * 1024),
        )(transfer_coef, group_order, member_order, active_mask, volume)

    in_specs = (P("grp", "mem", None, None, None), P(), P(), P(), P("grp", "mem"))
    out_specs = P(None, "mem", "grp")
    return jax.shard_map(body, mesh=mesh, in_specs=in_specs, out_specs=out_specs, check_vma=False)
```

```python
import functools
import math

import jax
import jax.numpy as jnp
from jax import lax
from jax.experimental import pallas as pl
from jax.experimental.pallas import tpu as pltpu
from jax.sharding import PartitionSpec as P

MESH = pl.DeviceIdType.MESH
CHUNKS = 8
EARLY = 6
TILE_ROWS = 8


def kernel(groups, members, coef_ref, group_ref, member_ref, active_ref, volume_ref, out_ref,
           vol, tloc, tin, col, pcol, mout, min_, tnear, tslab, sout, sin, zout, zin,
           vol_sem, t_send, t_recv, c_send, c_recv, m_send, m_recv, s_send, s_recv, z_send, z_recv):
    chunks, _, samples, rows, cols = vol.shape
    block_rows = chunks * rows
    chips = members // 2
    group_cols = cols // groups
    g = lax.axis_index("grp")
    me = lax.axis_index("mem")
    chip = me // 2
    core = me % 2
    partner = me + 1 - 2 * core
    row_tiles = rows // TILE_ROWS

    def fetch(j, d):
        start = pl.multiple_of(d * block_rows + j * rows, TILE_ROWS)
        return pltpu.make_async_copy(
            volume_ref.at[0, 0, :, pl.ds(start, rows), :], vol.at[j, d], vol_sem.at[j])

    def send_t(j, d, src):
        return pltpu.make_async_remote_copy(
            tloc.at[j, d], tin.at[j, src], t_send, t_recv.at[j],
            device_id={"mem": d}, device_id_type=MESH)

    def send_col(j, k):
        return pltpu.make_async_remote_copy(
            col.at[j, 2 * k + 1 - core], pcol.at[j, k], c_send, c_recv.at[j],
            device_id={"mem": partner}, device_id_type=MESH)

    def send_m(j, k, src):
        return pltpu.make_async_remote_copy(
            mout.at[j, k], min_.at[j, src], m_send, m_recv.at[j],
            device_id={"mem": 2 * k + core}, device_id_type=MESH)

    def send_s(j, k, src):
        return pltpu.make_async_remote_copy(
            sout.at[j, k], sin.at[j, src], s_send, s_recv.at[j],
            device_id={"mem": 2 * k + core}, device_id_type=MESH)

    def send_z(j, k, src):
        return pltpu.make_async_remote_copy(
            zout.at[j, k], zin.at[j, src], z_send, z_recv.at[j],
            device_id={"grp": k}, device_id_type=MESH)

    def landed(ref, sem):
        pltpu.make_async_copy(ref, ref, sem).wait()

    def each(count, fn):
        def step(i, carry):
            fn(i)
            return carry
        lax.fori_loop(0, count, step, 0)

    each(chunks, lambda j: each(members, lambda off: fetch(j, (me + 1 + off) % members).start()))

    barrier = pltpu.get_barrier_semaphore()
    each(members - 1, lambda off: pl.semaphore_signal(
        barrier, inc=1, device_id={"mem": (me + 1 + off) % members}, device_id_type=MESH))
    each(groups - 1, lambda off: pl.semaphore_signal(
        barrier, inc=1, device_id={"grp": (g + 1 + off) % groups}, device_id_type=MESH))

    density_factor = math.sqrt(3.0 / (samples * groups * members) * math.log2(math.e))
    coef = [[coef_ref[c, p] * (0.5 if c < 3 else density_factor) for p in range(4)] for c in range(4)]
    active = active_ref[0, 0].astype(jnp.float32)
    half_active = active * 0.5
    width = min(512, cols)
    col_tiles = cols // width
    ranks = [member_ref[g, i] for i in range(members)]
    near = [jnp.minimum(ranks[2 * q], ranks[2 * q + 1]) for q in range(chips)]
    far = [jnp.maximum(ranks[2 * q], ranks[2 * q + 1]) for q in range(chips)]
    own_first = member_ref[g, me] < member_ref[g, partner]
    orders = [group_ref[i] for i in range(groups)]

    def tiles(fn, count=None):
        def step(i, carry):
            row = pl.ds(pl.multiple_of((i // col_tiles) * TILE_ROWS, TILE_ROWS), TILE_ROWS)
            column = pl.ds(pl.multiple_of((i % col_tiles) * width, width), width)
            fn(row, column)
            return carry
        lax.fori_loop(0, row_tiles * col_tiles, step, 0)

    def march(j, d):
        def tile(row, column):
            depth = jnp.zeros((TILE_ROWS, width), jnp.float32)
            light = jnp.ones((TILE_ROWS, width), jnp.float32)
            colour = [jnp.zeros((TILE_ROWS, width), jnp.float32) for _ in range(3)]
            for k in range(samples):
                v = vol[j, d, k, row, column]
                poly = [q[0] + v * (q[1] + v * (q[2] + v * q[3])) for q in coef]
                depth = depth - poly[3] * poly[3]
                after = jnp.exp2(depth)
                weight = light - after
                light = after
                colour = [colour[c] + weight * jnp.tanh(poly[c]) for c in range(3)]
            coverage = 1.0 - light
            tloc[j, d, row, column] = 1.0 - active * coverage
            for c in range(3):
                col[j, d, c, row, column] = half_active * (coverage + colour[c])
        tiles(tile)

    early = min(EARLY, members - 1)

    def produce(j):
        @pl.when(j > 0)
        def _():
            landed(vol.at[j], vol_sem.at[j])

        def unit(off):
            d = (me + 1 + off) % members

            @pl.when(jnp.logical_or(j > 0, off >= early))
            def _():
                march(j, d)

            @pl.when(off < members - 1)
            def _():
                send_t(j, d, me).start()

            @pl.when(d % 2 != core)
            def _():
                send_col(j, d // 2).start()
        each(members, unit)

        def keep(row, column):
            tin[j, me, row, column] = tloc[j, me, row, column]
        tiles(keep)

    def ratios(j):
        landed(tin.at[j, pl.ds(0, members - 1)], t_recv.at[j])

        def tile(row, column):
            t = [tin[j, i, row, column] for i in range(members)]
            total = t[0]
            for i in range(1, members):
                total = total * t[i]
            tslab[j, row, column] = total
            for q in range(chips):
                before = jnp.ones((TILE_ROWS, width), jnp.float32)
                between = jnp.ones((TILE_ROWS, width), jnp.float32)
                for i in range(members):
                    nearer = ranks[i] < near[q]
                    inside = jnp.logical_and(ranks[i] >= near[q], ranks[i] < far[q])
                    before = before * jnp.where(nearer, t[i], 1.0)
                    between = between * jnp.where(inside, t[i], 1.0)
                tnear[j, q, row, column] = before
                mout[j, q, row, column] = between
        tiles(tile)
        each(chips - 1, lambda off: send_m(j, (chip + 1 + off) % chips, chip).start())

        def keep(row, column):
            min_[j, chip, row, column] = mout[j, chip, row, column]
        tiles(keep)

    def pair_sums(j):
        landed(min_.at[j, pl.ds(0, chips - 1)], m_recv.at[j])
        landed(pcol.at[j], c_recv.at[j])

        def unit(off):
            k = (chip + 1 + off) % chips

            def tile(row, column):
                ratio = min_[j, k, row, column]
                own_factor = jnp.where(own_first, 1.0, ratio)
                other_factor = jnp.where(own_first, ratio, 1.0)
                for c in range(3):
                    sout[j, k, c, row, column] = (
                        col[j, 2 * k + core, c, row, column] * own_factor
                        + pcol[j, k, c, row, column] * other_factor)
            tiles(tile)

            @pl.when(off < chips - 1)
            def _():
                send_s(j, k, chip).start()
        each(chips, unit)

        def keep(row, column):
            for c in range(3):
                sin[j, chip, c, row, column] = sout[j, chip, c, row, column]
        tiles(keep)

    def slab(j):
        landed(sin.at[j, pl.ds(0, chips - 1)], s_recv.at[j])

        def part(k):
            def tile(i):
                row = pl.ds(pl.multiple_of(i * TILE_ROWS, TILE_ROWS), TILE_ROWS)
                column = pl.ds(pl.multiple_of(k * group_cols, group_cols), group_cols)
                factor = [tnear[j, q, row, column] for q in range(chips)]
                for c in range(3):
                    total = factor[0] * sin[j, 0, c, row, column]
                    for q in range(1, chips):
                        total = total + factor[q] * sin[j, q, c, row, column]
                    zout[j, k, c, row, :] = total
                zout[j, k, 3, row, :] = tslab[j, row, column]
            each(row_tiles, tile)

        def unit(off):
            k = (g + 1 + off) % groups
            part(k)

            @pl.when(off < groups - 1)
            def _():
                send_z(j, k, g).start()
        each(groups, unit)
        zin[j, g] = zout[j, g]

    def finish(j):
        landed(zin.at[j, pl.ds(0, groups - 1)], z_recv.at[j])
        for r in range(row_tiles):
            row = pl.ds(r * TILE_ROWS, TILE_ROWS)
            out_row = pl.ds(pl.multiple_of(j * rows + r * TILE_ROWS, TILE_ROWS), TILE_ROWS)
            t = [zin[j, i, 3, row, :] for i in range(groups)]
            total = t[0]
            for i in range(1, groups):
                total = total * t[i]
            out_ref[3, out_row, :] = 1.0 - total
            factor = []
            for i in range(groups):
                before = jnp.ones_like(total)
                for o in range(groups):
                    if o != i:
                        before = before * jnp.where(orders[o] < orders[i], t[o], 1.0)
                factor.append(before)
            for c in range(3):
                colour = factor[0] * zin[j, 0, c, row, :]
                for i in range(1, groups):
                    colour = colour + factor[i] * zin[j, i, c, row, :]
                out_ref[c, out_row, :] = colour

    def step(s):
        for lag, stage in enumerate((produce, ratios, pair_sums, slab, finish)):
            @pl.when(jnp.logical_and(s >= lag, s < chunks + lag))
            def _():
                stage(s - lag)
    landed(vol.at[0], vol_sem.at[0])
    each(early, lambda off: march(0, (me + 1 + off) % members))
    pl.semaphore_wait(barrier, members + groups - 2)
    each(chunks + 4, step)

    landed(tloc.at[:, pl.ds(0, members - 1)], t_send)
    landed(pcol, c_send)
    landed(mout.at[:, pl.ds(0, chips - 1)], m_send)
    landed(sout.at[:, pl.ds(0, chips - 1)], s_send)
    landed(zout.at[:, pl.ds(0, groups - 1)], z_send)


def solution(mesh):
    groups, members = mesh.shape["grp"], mesh.shape["mem"]
    chips = members // 2

    def body(volume, transfer_coef, group_order, member_order, active_mask):
        samples, image_rows, cols = volume.shape[2:]
        block_rows = image_rows // members
        chunks = min(CHUNKS, block_rows // TILE_ROWS)
        rows = block_rows // chunks
        group_cols = cols // groups
        smem = pl.BlockSpec(memory_space=pltpu.SMEM)
        f32 = jnp.float32
        dma = pltpu.SemaphoreType.DMA
        scratch = [
            pltpu.VMEM((chunks, members, samples, rows, cols), f32),
            pltpu.VMEM((chunks, members, rows, cols), f32),
            pltpu.VMEM((chunks, members, rows, cols), f32),
            pltpu.VMEM((chunks, members, 3, rows, cols), f32),
            pltpu.VMEM((chunks, chips, 3, rows, cols), f32),
            pltpu.VMEM((chunks, chips, rows, cols), f32),
            pltpu.VMEM((chunks, chips, rows, cols), f32),
            pltpu.VMEM((chunks, chips, rows, cols), f32),
            pltpu.VMEM((chunks, rows, cols), f32),
            pltpu.VMEM((chunks, chips, 3, rows, cols), f32),
            pltpu.VMEM((chunks, chips, 3, rows, cols), f32),
            pltpu.VMEM((chunks, groups, 4, rows, group_cols), f32),
            pltpu.VMEM((chunks, groups, 4, rows, group_cols), f32),
            dma((chunks,)),
            dma, dma((chunks,)),
            dma, dma((chunks,)),
            dma, dma((chunks,)),
            dma, dma((chunks,)),
            dma, dma((chunks,)),
        ]
        return pl.pallas_call(
            functools.partial(kernel, groups, members),
            out_shape=jax.ShapeDtypeStruct((4, block_rows, group_cols), f32),
            in_specs=[smem, smem, smem, smem, pl.BlockSpec(memory_space=pl.ANY)],
            out_specs=pl.BlockSpec(memory_space=pltpu.VMEM),
            scratch_shapes=scratch,
            compiler_params=pltpu.CompilerParams(
                collective_id=0, has_side_effects=True, vmem_limit_bytes=60 * 1024 * 1024),
        )(transfer_coef, group_order, member_order, active_mask, volume)

    in_specs = (P("grp", "mem", None, None, None), P(), P(), P(), P("grp", "mem"))
    out_specs = P(None, "mem", "grp")
    return jax.shard_map(body, mesh=mesh, in_specs=in_specs, out_specs=out_specs, check_vma=False)
```
